32 devices in a mesh: outer: 4 (over y, core), inner: 8 (over z, x).
Axes of the slice: x: 2, y: 2, z: 4, core: 2. Of those that a mesh axis runs over, the one named last changes fastest.
Arguments:
- queries: bfloat16 [16384, 16, 128], P(('outer', 'inner')), may hold values from -1.5 to 1.5
- key_vectors: bfloat16 [16384, 16, 128], P(('outer', 'inner')), may hold values from -1.5 to 1.5
- value_vectors: bfloat16 [16384, 16, 128], P(('outer', 'inner')), may hold values from -6 to 6
- level_weights: float32 [18, 16, 16384], P(None, None, ('outer', 'inner')), may hold values from 0.25 to 1
Outputs:
- attended: bfloat16 [16384, 16, 128], P(('outer', 'inner'))
The draws below stay inside these ranges and needn't reach their ends.
All inputs are finite; a program needn't handle non-finite values.
Results may differ from the reference program's by a relative error of at most 0.0049.
Values may be sent and summed in bfloat16 or wider, within the bound.
No kernel may reach another device: no remote copies, remote signals or barrier semaphores. Data moves between devices by JAX's collectives and lax.ppermute only.
A program may use at most 128 MiB of HBM per device.

```python
import math
import jax
import jax.numpy as jnp
from jax import lax

HEADS = 16
HDIM = 128
LEVELS = 18
TOK_BITS = 9
TOK_DEV = 512
TOKENS = 16384


def level_of(own_key, shape, split, low, top_value):
    loudness = 1.0
    for dim, shards_of in split:
        steps = jax.random.uniform(jax.random.fold_in(jax.random.fold_in(own_key, 6), dim), (shards_of,), jnp.float32, low / len(split), top_value / len(split))
        loudness = loudness * jnp.repeat(jnp.exp(steps), shape[dim] // shards_of).reshape((-1,) + (1,) * (len(shape) - 1 - dim))
    return loudness


def normal_values(stream_key, dims, deviation, most, shards=(), kind=jnp.bfloat16):
    factor_of = level_of(stream_key, dims, shards, -0.22, 0.18) if shards else 1.0
    values = jax.random.normal(stream_key, dims, jnp.float32) * deviation * factor_of
    return jnp.minimum(jnp.maximum(values, -most), most).astype(kind)


def setup_inputs(seed: int = 0) -> dict:
    keys = jax.random.split(jax.random.key(seed), 5)
    queries = normal_values(keys[0], (TOKENS, HEADS, HDIM), 0.25, 1.5, ((0, 32),))
    key_vectors = normal_values(keys[1], (TOKENS, HEADS, HDIM), 0.25, 1.5, ((0, 32),))
    value_vectors = normal_values(keys[2], (TOKENS, HEADS, HDIM), 1.0, 6.0, ((0, 32),))
    level_weights = jnp.clip(jnp.exp(math.log(1.0) - 1.3862944 * jax.random.uniform(keys[3], (LEVELS, HEADS, TOKENS), jnp.float32) ** level_of(keys[3], (LEVELS, HEADS, TOKENS), ((2, 32),), -0.2, 0.2)), 0.25, 1.0)
    return dict(queries=queries, key_vectors=key_vectors, value_vectors=value_vectors, level_weights=level_weights)


def level_table(block_len):
    position = jnp.arange(block_len, dtype=jnp.int32)
    differ = position[:, None] ^ position[None, :]
    levels_at = jnp.zeros((block_len, block_len), jnp.int32)
    for bit_pos in range(block_len.bit_length() - 1):
        levels_at = levels_at + (differ >= (1 << bit_pos)).astype(jnp.int32)
    causal = position[None, :] <= position[:, None]
    return levels_at, causal


def scaled_gains(level_weights):
    count = level_weights.shape[0]
    factor = jnp.exp2(-0.5 * jnp.arange(count, dtype=jnp.float32))
    return level_weights * factor[:, None, None]


def local_terms(queries, key_vectors, value_vectors, gains):
    block_len = queries.shape[0]
    levels_at, causal = level_table(block_len)
    scores = jnp.einsum("thd,shd->hts", queries.astype(jnp.float32), key_vectors.astype(jnp.float32))
    weighting = jnp.zeros(scores.shape, jnp.float32)
    for level_idx in range(block_len.bit_length()):
        weighting = weighting + jnp.where((levels_at == level_idx)[None], gains[level_idx][:, :, None], jnp.float32(0.0))
    attn_weights = jnp.where(causal[None], scores * weighting, jnp.float32(0.0)).astype(jnp.bfloat16)
    return jnp.einsum("hts,shd->thd", attn_weights.astype(jnp.float32), value_vectors.astype(jnp.float32))


def reference(queries, key_vectors, value_vectors, level_weights):
    blocks = TOKENS // TOK_DEV
    depth = (blocks - 1).bit_length()
    gains = scaled_gains(level_weights)
    q_blocks = queries.reshape(blocks, TOK_DEV, HEADS, HDIM)
    k_blocks = key_vectors.reshape(blocks, TOK_DEV, HEADS, HDIM)
    v_blocks = value_vectors.reshape(blocks, TOK_DEV, HEADS, HDIM)
    gain_blocks = gains.reshape(LEVELS, HEADS, blocks, TOK_DEV).transpose(2, 0, 1, 3)

    def block_state(pair):
        return jnp.einsum("shd,she->hde", pair[0].astype(jnp.float32), pair[1].astype(jnp.float32))

    tiers = [lax.map(block_state, (k_blocks, v_blocks))]
    for step_idx in range(depth - 1):
        lower = tiers[-1]
        tiers.append(lower[0::2] + lower[1::2])

    def one_block(inputs):
        place, q_blk, k_blk, v_blk, gain_blk = inputs
        output_sum = local_terms(q_blk, k_blk, v_blk, gain_blk)
        for bit_pos in range(depth):
            switch = ((place >> bit_pos) & 1).astype(jnp.float32)
            sibling = ((place >> bit_pos) ^ 1).astype(jnp.int32)
            bucket = lax.dynamic_index_in_dim(tiers[bit_pos], sibling, 0, keepdims=False).astype(jnp.bfloat16)
            contrib = jnp.einsum("thd,hde->the", q_blk.astype(jnp.float32), bucket.astype(jnp.float32))
            level_gain = gain_blk[TOK_BITS + 1 + bit_pos] * switch
            output_sum = output_sum + contrib * level_gain.T[:, :, None]
        return output_sum.astype(jnp.bfloat16)

    places = jnp.arange(blocks, dtype=jnp.int32)
    result = lax.map(one_block, (places, q_blocks, k_blocks, v_blocks, gain_blocks))
    return result.reshape(TOKENS, HEADS, HDIM)
```

```python
import functools
import jax
import jax.numpy as jnp
from jax import lax
from jax.experimental import pallas as pl
from jax.sharding import PartitionSpec as P

AXES = ("outer", "inner")
HEAD_BLOCK = 8
F32, BF16 = jnp.float32, jnp.bfloat16


def dot_nt(a, b):
    return lax.dot_general(a, b, (((1,), (1,)), ((), ())), preferred_element_type=F32)


def state_kernel(k_ref, v_ref, state_ref, first_ref):
    half = k_ref.shape[0] // 2
    keys = jnp.swapaxes(k_ref[...], 0, 1)
    values = jnp.swapaxes(v_ref[...], 0, 1)
    for h in range(keys.shape[0]):
        turned = values[h].T
        first = jnp.dot(turned[:, :half], keys[h, :half], preferred_element_type=F32)
        rest = jnp.dot(turned[:, half:], keys[h, half:], preferred_element_type=F32)
        first_ref[h] = first.astype(BF16)
        state_ref[h] = (first + rest).astype(BF16)


def block_states(key_vectors, value_vectors):
    tokens, heads, dim = key_vectors.shape
    source = pl.BlockSpec((tokens, HEAD_BLOCK, dim), lambda i: (0, i, 0))
    target = pl.BlockSpec((HEAD_BLOCK, dim, dim), lambda i: (i, 0, 0))
    shape = jax.ShapeDtypeStruct((heads, dim, dim), BF16)
    return pl.pallas_call(
        state_kernel,
        grid=(heads // HEAD_BLOCK,),
        in_specs=[source, source],
        out_specs=[target, target],
        out_shape=[shape, shape],
        name="states",
        cost_estimate=pl.CostEstimate(
            flops=2 * tokens * heads * dim * dim,
            bytes_accessed=4 * tokens * heads * dim,
            transcendentals=0,
        ),
    )(key_vectors, value_vectors)


def local_kernel(second, q_ref, k_ref, v_ref, w_ref, first_ref, acc_ref, qh_ref):
    tile = q_ref.shape[0]
    depth = tile.bit_length() - 1
    groups = tile // 8
    queries = jnp.swapaxes(q_ref[...], 0, 1)
    keys = jnp.swapaxes(k_ref[...], 0, 1)
    values = jnp.swapaxes(v_ref[...], 0, 1)
    lane = lax.broadcasted_iota(jnp.int32, (8, tile), 1)
    row = lax.broadcasted_iota(jnp.int32, (8, tile), 0)
    fine = (lane & 7) ^ row
    fine_ok = row <= (lane & 7)
    group_lane = lax.broadcasted_iota(jnp.int32, (groups, tile), 1) >> 3
    group_row = lax.broadcasted_iota(jnp.int32, (groups, tile), 0)
    coarse = jnp.where(group_row < group_lane, group_lane ^ group_row, 0)
    for h in range(queries.shape[0]):
        gain = [w_ref[l, h : h + 1, :] * (2.0 ** (-0.5 * l)) for l in range(depth + 2)]
        near = jnp.where(fine == 0, gain[0], 0.0)
        for l in range(1, 4):
            near = jnp.where((fine >> (l - 1)) == 1, gain[l], near)
        near = jnp.where(fine_ok, near, 0.0)
        far = jnp.zeros((groups, tile), F32)
        for l in range(4, depth + 1):
            far = jnp.where((coarse >> (l - 4)) == 1, gain[l], far)
        scores = dot_nt(keys[h], queries[h])
        rows = []
        for g in range(0, groups, 2):
            pair = [
                jnp.where(
                    (lane >> 3) == g + i,
                    near,
                    jnp.broadcast_to(far[g + i : g + i + 1, :], (8, tile)),
                )
                * scores[8 * (g + i) : 8 * (g + i) + 8, :]
                for i in range(2)
            ]
            rows.append(jnp.concatenate(pair, axis=0).astype(BF16))
        weights = jnp.concatenate(rows, axis=0)
        out = jnp.dot(values[h].T, weights, preferred_element_type=F32)
        if second:
            out = out + gain[depth + 1] * dot_nt(first_ref[h], queries[h])
        acc_ref[h] = out
        qh_ref[h] = queries[h]


def local_part(half, queries, key_vectors, value_vectors, level_weights, first):
    tokens, heads, dim = queries.shape
    tile = tokens // 2
    levels = tile.bit_length() + 1
    source = pl.BlockSpec((tile, HEAD_BLOCK, dim), lambda i: (half, i, 0))
    return pl.pallas_call(
        functools.partial(local_kernel, half == 1),
        grid=(heads // HEAD_BLOCK,),
        in_specs=[
            source,
            source,
            source,
            pl.BlockSpec((levels, HEAD_BLOCK, tile), lambda i: (0, i, half)),
            pl.BlockSpec((HEAD_BLOCK, dim, dim), lambda i: (i, 0, 0)),
        ],
        out_specs=[
            pl.BlockSpec((HEAD_BLOCK, dim, tile), lambda i: (i, 0, 0)),
            pl.BlockSpec((HEAD_BLOCK, tile, dim), lambda i: (i, 0, 0)),
        ],
        out_shape=[
            jax.ShapeDtypeStruct((heads, dim, tile), F32),
            jax.ShapeDtypeStruct((heads, tile, dim), BF16),
        ],
        cost_estimate=pl.CostEstimate(
            flops=4 * tile * tile * heads * dim,
            bytes_accessed=12 * tile * heads * dim,
            transcendentals=0,
        ),
    )(queries, key_vectors, value_vectors, level_weights, first)


def merge_kernel(count, qh_ref, acc_ref, w_ref, *rest):
    out_ref = rest[count]
    for h in range(qh_ref.shape[0]):
        total = acc_ref[h]
        for n in range(count):
            total = total + w_ref[n, h : h + 1, :] * dot_nt(rest[n][h], qh_ref[h])
        out_ref[h] = total


def merge_part(half, turned, acc, gains, buckets):
    heads, tile, dim = turned.shape
    count = len(buckets)
    return pl.pallas_call(
        functools.partial(merge_kernel, count),
        grid=(heads // HEAD_BLOCK,),
        in_specs=[
            pl.BlockSpec((HEAD_BLOCK, tile, dim), lambda i: (i, 0, 0)),
            pl.BlockSpec((HEAD_BLOCK, dim, tile), lambda i: (i, 0, 0)),
            pl.BlockSpec((count, HEAD_BLOCK, tile), lambda i: (0, i, half)),
        ]
        + [pl.BlockSpec((HEAD_BLOCK, dim, dim), lambda i: (i, 0, 0))] * count,
        out_specs=pl.BlockSpec((HEAD_BLOCK, dim, tile), lambda i: (i, 0, 0)),
        out_shape=jax.ShapeDtypeStruct((heads, dim, tile), F32),
        input_output_aliases={1: 0},
        cost_estimate=pl.CostEstimate(
            flops=2 * count * tile * heads * dim * dim,
            bytes_accessed=10 * tile * heads * dim,
            transcendentals=0,
        ),
    )(turned, acc, gains, *buckets)


def final_kernel(count, q0_ref, q1_ref, a0_ref, a1_ref, w_ref, *rest):
    out_ref = rest[count]

    def side(q_ref, a_ref):
        done = []
        for h in range(q_ref.shape[0]):
            total = a_ref[h]
            for n in range(count):
                total = total + w_ref[n, h : h + 1, :] * dot_nt(rest[n][h], q_ref[h])
            done.append(total.T.astype(BF16))
        out_ref[...] = jnp.swapaxes(jnp.stack(done), 0, 1)

    which = pl.program_id(0)
    pl.when(which == 0)(lambda: side(q0_ref, a0_ref))
    pl.when(which == 1)(lambda: side(q1_ref, a1_ref))


def final_part(turned, accs, gains, buckets):
    heads, tile, dim = turned[0].shape
    count = len(buckets)
    blocks = heads // HEAD_BLOCK
    first = lambda s, i: (jnp.where(s == 0, i, blocks - 1), 0, 0)
    last = lambda s, i: (jnp.where(s == 1, i, 0), 0, 0)
    return pl.pallas_call(
        functools.partial(final_kernel, count),
        grid=(2, blocks),
        in_specs=[
            pl.BlockSpec((HEAD_BLOCK, tile, dim), first),
            pl.BlockSpec((HEAD_BLOCK, tile, dim), last),
            pl.BlockSpec((HEAD_BLOCK, dim, tile), first),
            pl.BlockSpec((HEAD_BLOCK, dim, tile), last),
            pl.BlockSpec((count, HEAD_BLOCK, tile), lambda s, i: (0, i, s)),
        ]
        + [pl.BlockSpec((HEAD_BLOCK, dim, dim), lambda s, i: (i, 0, 0))] * count,
        out_specs=pl.BlockSpec((tile, HEAD_BLOCK, dim), lambda s, i: (s, i, 0)),
        out_shape=jax.ShapeDtypeStruct((2 * tile, heads, dim), BF16),
        name="final",
        cost_estimate=pl.CostEstimate(
            flops=4 * count * tile * heads * dim * dim,
            bytes_accessed=16 * tile * heads * dim,
            transcendentals=0,
        ),
    )(*turned, *accs, gains, *buckets)


def exchange(value, mask, keep=None):
    total = lax.axis_size("outer") * lax.axis_size("inner")
    pairs = [(i, i ^ mask) for i in range(total) if keep is None or keep(i ^ mask)]
    return lax.ppermute(value, AXES, pairs)


def exchange_states(state, place, inner_depth, depth):
    quarter = state.shape[0] // 4
    rank = place & 3
    part = lambda r: lax.dynamic_slice_in_dim(state, r * quarter, quarter, 0)
    got = {m: exchange(part(rank ^ m), m) for m in (3, 2, 1)}
    buckets = {0: exchange(state, 1, lambda d: d & 1 == 1)}
    mine = part(rank).astype(F32) + got[1].astype(F32)
    other = got[2].astype(F32) + got[3].astype(F32)
    high, odd = (rank >> 1) == 1, (rank & 1) == 1
    pieces = {1: jnp.where(high, other, mine).astype(BF16)}
    total = mine + other
    for g in range(2, depth):
        pieces[g] = exchange(total.astype(BF16), 1 << g)
        total = total + pieces[g].astype(F32)

    def gather_late(g):
        a = pieces[g]
        b = exchange(a, 2)
        pair = jnp.stack([jnp.where(high, b, a), jnp.where(high, a, b)])
        twin = exchange(pair, 1)
        both = jnp.stack([jnp.where(odd, twin, pair), jnp.where(odd, pair, twin)], 1)
        return both.reshape(state.shape)

    low, top = inner_depth, depth - 1
    for g in range(1, depth):
        if g not in (low, top):
            buckets[g] = gather_late(g)
    upper = (place >> low & 1) == 1
    chosen = jnp.where(upper, pieces[low], pieces[top])
    full = jnp.zeros((4,) + chosen.shape, BF16)
    full = lax.dynamic_update_slice_in_dim(full, chosen[None], rank, 0)
    for m in (3, 2, 1):
        piece = exchange(chosen, m)
        full = lax.dynamic_update_slice_in_dim(full, piece[None], rank ^ m, 0)
    full = full.reshape(state.shape)
    handed = exchange(full, 1 << low, lambda d: d >> low & 1 == 1)
    buckets[low] = full
    buckets[top] = jnp.where(upper, handed, full)
    return [buckets[g] for g in range(depth)]


def per_device(queries, key_vectors, value_vectors, level_weights):
    inner_count = lax.axis_size("inner")
    inner_depth = inner_count.bit_length() - 1
    depth = inner_depth + lax.axis_size("outer").bit_length() - 1
    place = lax.axis_index("outer") * inner_count + lax.axis_index("inner")
    local_depth = queries.shape[0].bit_length() - 1
    state, first = block_states(key_vectors, value_vectors)
    buckets = exchange_states(state, place, inner_depth, depth)
    bits = jnp.arange(depth)
    factor = jnp.exp2(-0.5 * (local_depth + 1 + bits).astype(F32))
    factor = factor * (place >> bits & 1).astype(F32)
    gains = level_weights[local_depth + 1 : local_depth + 1 + depth] * factor[:, None, None]
    turned, accs = [], []
    late = (inner_depth, depth - 1)
    early = [g for g in range(depth) if g not in late]
    pick = lambda order: jnp.stack([gains[g] for g in order])
    for half in range(2):
        acc, flat = local_part(
            half, queries, key_vectors, value_vectors, level_weights, first
        )
        accs.append(merge_part(half, flat, acc, pick(early), [buckets[g] for g in early]))
        turned.append(flat)
    return final_part(turned, accs, pick(late), [buckets[g] for g in late])


def solution(mesh):
    placed = P(AXES, None, None)
    return jax.shard_map(
        per_device,
        mesh=mesh,
        in_specs=(placed, placed, placed, P(None, None, AXES)),
        out_specs=placed,
        check_vma=False,
    )
```

```python
import functools
import jax
import jax.numpy as jnp
from jax import lax
from jax.experimental import pallas as pl
from jax.experimental.pallas import tpu as pltpu
from jax.sharding import PartitionSpec as P

AXES = ("outer", "inner")
HEAD_BLOCK = 8
STATE_VMEM = 9 << 20
LOCAL_VMEM = 9 << 20
FINAL_VMEM = 12 << 20
F32, BF16 = jnp.float32, jnp.bfloat16


def dot_nt(a, b):
    return lax.dot_general(a, b, (((1,), (1,)), ((), ())), preferred_element_type=F32)


def scalar_grid(grid, in_specs, out_specs):
    return pltpu.PrefetchScalarGridSpec(
        num_scalar_prefetch=1, grid=grid, in_specs=in_specs, out_specs=out_specs
    )


def state_kernel(place_ref, k_ref, v_ref, state_ref, first_ref):
    half = k_ref.shape[0] // 2
    quarter = k_ref.shape[1] // 2
    flip = place_ref[0] & 1
    keys = jnp.swapaxes(k_ref[...], 0, 1)
    values = jnp.swapaxes(v_ref[...], 0, 1)
    for h in range(2 * quarter):
        turned = values[h].T
        first = jnp.dot(turned[:, :half], keys[h, :half], preferred_element_type=F32)
        rest = jnp.dot(turned[:, half:], keys[h, half:], preferred_element_type=F32)
        first_ref[h] = first.astype(BF16)
        state_ref[(h // quarter ^ flip) * quarter + h % quarter] = (first + rest).astype(BF16)


def block_states(place, key_vectors, value_vectors):
    tokens, heads, dim = key_vectors.shape
    block = heads // 2
    source = pl.BlockSpec((tokens, block, dim), lambda i, p: (0, i ^ (p[0] >> 1 & 1), 0))
    shape = jax.ShapeDtypeStruct((heads, dim, dim), BF16)
    return pl.pallas_call(
        state_kernel,
        grid_spec=scalar_grid(
            (2,),
            [source, source],
            [
                pl.BlockSpec((block, dim, dim), lambda i, p: (i, 0, 0)),
                pl.BlockSpec((block, dim, dim), lambda i, p: (i ^ (p[0] >> 1 & 1), 0, 0)),
            ],
        ),
        out_shape=[shape, shape],
        name="states",
        compiler_params=pltpu.CompilerParams(vmem_limit_bytes=STATE_VMEM),
        cost_estimate=pl.CostEstimate(
            flops=2 * tokens * heads * dim * dim,
            bytes_accessed=4 * tokens * heads * dim,
            transcendentals=0,
        ),
    )(place, key_vectors, value_vectors)


def local_kernel(second, q_ref, k_ref, v_ref, w_ref, first_ref, acc_ref, qh_ref):
    tile = q_ref.shape[0]
    depth = tile.bit_length() - 1
    groups = tile // 8
    queries = jnp.swapaxes(q_ref[...], 0, 1)
    keys = jnp.swapaxes(k_ref[...], 0, 1)
    values = jnp.swapaxes(v_ref[...], 0, 1)
    heads = queries.shape[0]
    lane = lax.broadcasted_iota(jnp.int32, (8, tile), 1)
    row = lax.broadcasted_iota(jnp.int32, (8, tile), 0)
    fine = (lane & 7) ^ row
    fine_ok = row <= (lane & 7)
    group_lane = lax.broadcasted_iota(jnp.int32, (groups, tile), 1) >> 3
    group_row = lax.broadcasted_iota(jnp.int32, (groups, tile), 0)
    coarse = jnp.where(group_row < group_lane, group_lane ^ group_row, 0)

    def gain(l, h):
        return w_ref[l, h : h + 1, :] * (2.0 ** (-0.5 * l))

    def weigh(h, scores):
        near = jnp.where(fine == 0, gain(0, h), 0.0)
        for l in range(1, 4):
            near = jnp.where((fine >> (l - 1)) == 1, gain(l, h), near)
        near = jnp.where(fine_ok, near, 0.0)
        far = jnp.zeros((groups, tile), F32)
        for l in range(4, depth + 1):
            far = jnp.where((coarse >> (l - 4)) == 1, gain(l, h), far)
        rows = []
        for g in range(0, groups, 2):
            pair = [
                jnp.where(
                    (lane >> 3) == g + i,
                    near,
                    jnp.broadcast_to(far[g + i : g + i + 1, :], (8, tile)),
                )
                * scores[8 * (g + i) : 8 * (g + i) + 8, :]
                for i in range(2)
            ]
            rows.append(jnp.concatenate(pair, axis=0).astype(BF16))
        return jnp.concatenate(rows, axis=0)

    scores, weights = {}, {}
    for h in range(heads + 2):
        if h < heads:
            scores[h] = dot_nt(keys[h], queries[h])
            qh_ref[h] = queries[h]
        if 0 <= h - 1 < heads:
            weights[h - 1] = weigh(h - 1, scores.pop(h - 1))
        if h - 2 >= 0:
            n = h - 2
            out = jnp.dot(values[n].T, weights.pop(n), preferred_element_type=F32)
            if second:
                out = out + gain(depth + 1, n) * dot_nt(first_ref[n], queries[n])
            acc_ref[n] = out


def local_part(half, queries, key_vectors, value_vectors, level_weights, first):
    tokens, heads, dim = queries.shape
    tile = tokens // 2
    levels = tile.bit_length() + 1
    source = pl.BlockSpec((tile, HEAD_BLOCK, dim), lambda i: (half, i, 0))
    return pl.pallas_call(
        functools.partial(local_kernel, half == 1),
        grid=(heads // HEAD_BLOCK,),
        in_specs=[
            source,
            source,
            source,
            pl.BlockSpec((levels, HEAD_BLOCK, tile), lambda i: (0, i, half)),
            pl.BlockSpec((HEAD_BLOCK, dim, dim), lambda i: (i, 0, 0)),
        ],
        out_specs=[
            pl.BlockSpec((HEAD_BLOCK, dim, tile), lambda i: (i, 0, 0)),
            pl.BlockSpec((HEAD_BLOCK, tile, dim), lambda i: (i, 0, 0)),
        ],
        out_shape=[
            pltpu.HBM((heads, dim, tile), F32),
            pltpu.HBM((heads, tile, dim), BF16),
        ],
        compiler_params=pltpu.CompilerParams(vmem_limit_bytes=LOCAL_VMEM),
        cost_estimate=pl.CostEstimate(
            flops=4 * tile * tile * heads * dim,
            bytes_accessed=12 * tile * heads * dim,
            transcendentals=0,
        ),
    )(queries, key_vectors, value_vectors, level_weights, first)


def bucket_sum(place, block, base, w_ref, q_ref, h, refs, rows):
    quarter = refs[0].shape[0] // 4
    spot = block * q_ref.shape[0] + h
    stack = [
        ref[(spot // quarter ^ (place & 3) ^ b) * quarter + spot % quarter]
        for ref, b in zip(refs, base)
    ]
    wide = dot_nt(jnp.concatenate(stack, axis=0), q_ref[h])
    dim = stack[0].shape[0]
    total = None
    for n, row in enumerate(rows):
        gain = sum(w_ref[l, h : h + 1, :] * c for l, c in row)
        part = wide[n * dim : (n + 1) * dim] * gain
        total = part if total is None else total + part
    return total


def final_kernel(meta, place_ref, q0_ref, q1_ref, a0_ref, a1_ref, w_ref, *rest):
    out_ref = rest[-1]
    refs = rest[:-1]
    base, local_depth, low, top = meta
    place = place_ref[0]
    bit = lambda g: (place >> g & 1).astype(F32)
    level = lambda g, c: (local_depth + 1 + g, c * 2.0 ** (-0.5 * (local_depth + 1 + g)))
    rows = [[level(g, bit(g))] for g in range(top) if g != low]
    rows.append([level(low, bit(low)), level(top, bit(top) * (1.0 - bit(low)))])
    rows.append([level(top, bit(top) * bit(low))])

    def side(q_ref, a_ref):
        done = []
        for h in range(q_ref.shape[0]):
            total = a_ref[h] + bucket_sum(
                place, pl.program_id(1), base, w_ref, q_ref, h, refs, rows
            )
            done.append(total.T.astype(BF16))
        out_ref[...] = jnp.swapaxes(jnp.stack(done), 0, 1)

    which = pl.program_id(0)
    pl.when(which == 0)(lambda: side(q0_ref, a0_ref))
    pl.when(which == 1)(lambda: side(q1_ref, a1_ref))


def final_part(place, turned, accs, level_weights, buckets, base, low, top):
    heads, tile, dim = turned[0].shape
    count = len(buckets)
    blocks = heads // HEAD_BLOCK
    first = lambda s, i, p: (jnp.where(s == 0, i, blocks - 1), 0, 0)
    last = lambda s, i, p: (jnp.where(s == 1, i, 0), 0, 0)
    return pl.pallas_call(
        functools.partial(final_kernel, (base, (2 * tile).bit_length() - 1, low, top)),
        grid_spec=scalar_grid(
            (2, blocks),
            [
                pl.BlockSpec((HEAD_BLOCK, tile, dim), first),
                pl.BlockSpec((HEAD_BLOCK, tile, dim), last),
                pl.BlockSpec((HEAD_BLOCK, dim, tile), first),
                pl.BlockSpec((HEAD_BLOCK, dim, tile), last),
                pl.BlockSpec(
                    (level_weights.shape[0], HEAD_BLOCK, tile), lambda s, i, p: (0, i, s)
                ),
            ]
            + [pl.BlockSpec((heads, dim, dim), lambda s, i, p: (0, 0, 0))] * count,
            pl.BlockSpec((tile, HEAD_BLOCK, dim), lambda s, i, p: (s, i, 0)),
        ),
        out_shape=jax.ShapeDtypeStruct((2 * tile, heads, dim), BF16),
        name="final",
        compiler_params=pltpu.CompilerParams(vmem_limit_bytes=FINAL_VMEM),
        cost_estimate=pl.CostEstimate(
            flops=4 * count * tile * heads * dim * dim,
            bytes_accessed=16 * tile * heads * dim,
            transcendentals=0,
        ),
    )(place, *turned, *accs, level_weights, *buckets)


def exchange(value, mask, keep=None):
    total = lax.axis_size("outer") * lax.axis_size("inner")
    pairs = [(i, i ^ mask) for i in range(total) if keep is None or keep(i ^ mask)]
    return lax.ppermute(value, AXES, pairs)


def exchange_states(state, place, inner_depth, depth):
    quarter = state.shape[0] // 4
    high = (place >> 1 & 1) == 1
    part = lambda m: state[m * quarter : (m + 1) * quarter]
    got = {m: exchange(part(m), m) for m in (3, 2, 1)}
    zero = exchange(state, 1, lambda d: d & 1 == 1)
    mine = part(0).astype(F32) + got[1].astype(F32)
    other = got[2].astype(F32) + got[3].astype(F32)
    total = mine + other
    sent = total.astype(BF16)
    pieces = {1: jnp.where(high, other, mine).astype(BF16)}
    pieces[1], sent, total = lax.optimization_barrier((pieces[1], sent, total))
    for g in range(2, depth):
        pieces[g] = exchange(sent, 1 << g)
        total = total + pieces[g].astype(F32)
        sent = total.astype(BF16)

    def gather_late(g):
        a = pieces[g]
        b = exchange(a, 2)
        twin = exchange(jnp.concatenate([a, b]), 1)
        return jnp.concatenate([a, twin[:quarter], b, twin[quarter:]])

    low, top = inner_depth, depth - 1
    buckets = [zero] + [gather_late(g) for g in range(1, top) if g != low]
    chosen = jnp.where((place >> low & 1) == 1, pieces[low], pieces[top])
    got = {m: exchange(chosen, m) for m in (3, 2, 1)}
    full = jnp.concatenate([chosen, got[1], got[2], got[3]])
    buckets.append(full)
    buckets.append(exchange(full, 1 << low, lambda d: d >> low & 1 == 1))
    return buckets


def per_device(queries, key_vectors, value_vectors, level_weights):
    inner_count = lax.axis_size("inner")
    inner_depth = inner_count.bit_length() - 1
    depth = inner_depth + lax.axis_size("outer").bit_length() - 1
    place = lax.axis_index("outer") * inner_count + lax.axis_index("inner")
    where = place.astype(jnp.int32).reshape(1)
    far = lambda x: pltpu.with_memory_space_constraint(x, pltpu.HBM)
    queries, key_vectors, value_vectors = map(far, (queries, key_vectors, value_vectors))
    state, first = block_states(where, key_vectors, value_vectors)
    buckets = exchange_states(state, place, inner_depth, depth)
    turned, accs = [], []
    for half in range(2):
        acc, flat = local_part(half, queries, key_vectors, value_vectors, level_weights, first)
        accs.append(pltpu.with_memory_space_constraint(acc, pltpu.HBM))
        turned.append(pltpu.with_memory_space_constraint(flat, pltpu.HBM))
    base = (1,) + (0,) * (len(buckets) - 1)
    return final_part(
        where, turned, accs, level_weights, buckets, base, inner_depth, depth - 1
    )


def solution(mesh):
    placed = P(AXES, None, None)
    return jax.shard_map(
        per_device,
        mesh=mesh,
        in_specs=(placed, placed, placed, P(None, None, AXES)),
        out_specs=placed,
        check_vma=False,
    )
```

```python
import functools
import jax
import jax.numpy as jnp
from jax import lax
from jax.experimental import pallas as pl
from jax.experimental.pallas import tpu as pltpu
from jax.sharding import PartitionSpec as P

AXES = ("outer", "inner")
HEAD_BLOCK = 8
STATE_VMEM = 14 << 20
LOCAL_VMEM = 14 << 20
MERGE_VMEM = 16 << 20
FINAL_VMEM = 14 << 20
MERGE_SPACE = pltpu.VMEM
SPLIT = 3
F32, BF16 = jnp.float32, jnp.bfloat16


def dot_nt(a, b):
    return lax.dot_general(a, b, (((1,), (1,)), ((), ())), preferred_element_type=F32)


def scalar_grid(grid, in_specs, out_specs):
    return pltpu.PrefetchScalarGridSpec(
        num_scalar_prefetch=1, grid=grid, in_specs=in_specs, out_specs=out_specs
    )


def state_kernel(place_ref, k_ref, v_ref, state_ref, first_ref):
    half = k_ref.shape[0] // 2
    quarter = k_ref.shape[1] // 2
    flip = place_ref[0] & 1
    keys = jnp.swapaxes(k_ref[...], 0, 1)
    values = jnp.swapaxes(v_ref[...], 0, 1)
    for h in range(2 * quarter):
        turned = values[h].T
        first = jnp.dot(turned[:, :half], keys[h, :half], preferred_element_type=F32)
        rest = jnp.dot(turned[:, half:], keys[h, half:], preferred_element_type=F32)
        spot = (h // quarter ^ flip) * quarter + h % quarter
        first_ref[spot] = first.astype(BF16)
        state_ref[spot] = (first + rest).astype(BF16)


def block_states(place, key_vectors, value_vectors):
    tokens, heads, dim = key_vectors.shape
    block = heads // 2
    source = pl.BlockSpec((tokens, block, dim), lambda i, p: (0, i ^ (p[0] >> 1 & 1), 0))
    shape = jax.ShapeDtypeStruct((heads, dim, dim), BF16)
    return pl.pallas_call(
        state_kernel,
        grid_spec=scalar_grid(
            (2,),
            [source, source],
            [pl.BlockSpec((block, dim, dim), lambda i, p: (i, 0, 0))] * 2,
        ),
        out_shape=[shape, shape],
        name="states",
        compiler_params=pltpu.CompilerParams(vmem_limit_bytes=STATE_VMEM),
        cost_estimate=pl.CostEstimate(
            flops=2 * tokens * heads * dim * dim,
            bytes_accessed=4 * tokens * heads * dim,
            transcendentals=0,
        ),
    )(place, key_vectors, value_vectors)


def local_kernel(start, blocks, place_ref, q_ref, k_ref, v_ref, w_ref, first_ref, acc_ref, qh_ref):
    unit = start + pl.program_id(0)
    second = (unit >= blocks).astype(F32)
    tile = q_ref.shape[0]
    depth = tile.bit_length() - 1
    groups = tile // 8
    queries = jnp.swapaxes(q_ref[...], 0, 1)
    keys = jnp.swapaxes(k_ref[...], 0, 1)
    values = jnp.swapaxes(v_ref[...], 0, 1)
    heads = queries.shape[0]
    lane = lax.broadcasted_iota(jnp.int32, (8, tile), 1)
    row = lax.broadcasted_iota(jnp.int32, (8, tile), 0)
    fine = (lane & 7) ^ row
    fine_ok = row <= (lane & 7)
    group_lane = lax.broadcasted_iota(jnp.int32, (groups, tile), 1) >> 3
    group_row = lax.broadcasted_iota(jnp.int32, (groups, tile), 0)
    coarse = jnp.where(group_row < group_lane, group_lane ^ group_row, 0)

    def gain(l, h):
        return w_ref[l, h : h + 1, :] * (2.0 ** (-0.5 * l))

    def weigh(h, scores):
        near = jnp.where(fine == 0, gain(0, h), 0.0)
        for l in range(1, 4):
            near = jnp.where((fine >> (l - 1)) == 1, gain(l, h), near)
        near = jnp.where(fine_ok, near, 0.0)
        far = jnp.zeros((groups, tile), F32)
        for l in range(4, depth + 1):
            far = jnp.where((coarse >> (l - 4)) == 1, gain(l, h), far)
        rows = []
        for g in range(0, groups, 2):
            pair = [
                jnp.where(
                    (lane >> 3) == g + i,
                    near,
                    jnp.broadcast_to(far[g + i : g + i + 1, :], (8, tile)),
                )
                * scores[8 * (g + i) : 8 * (g + i) + 8, :]
                for i in range(2)
            ]
            rows.append(jnp.concatenate(pair, axis=0).astype(BF16))
        return jnp.concatenate(rows, axis=0)

    scores, weights = {}, {}
    for h in range(heads + 2):
        if h < heads:
            scores[h] = dot_nt(keys[h], queries[h])
            qh_ref[h] = queries[h]
        if 0 <= h - 1 < heads:
            weights[h - 1] = weigh(h - 1, scores.pop(h - 1))
        if h - 2 >= 0:
            n = h - 2
            out = jnp.dot(values[n].T, weights.pop(n), preferred_element_type=F32)
            last = [(depth + 1, 2.0 ** (-0.5 * (depth + 1)) * second)]
            acc_ref[n] = out + bucket_sum(
                place_ref[0], unit % blocks, w_ref, queries, n, [first_ref], [last]
            )


def local_part(start, count, place, queries, key_vectors, value_vectors, level_weights, first):
    tokens, heads, dim = queries.shape
    tile = tokens // 2
    blocks = heads // HEAD_BLOCK
    source = pl.BlockSpec(
        (tile, HEAD_BLOCK, dim), lambda i, p: ((start + i) // blocks, (start + i) % blocks, 0)
    )
    return pl.pallas_call(
        functools.partial(local_kernel, start, blocks),
        grid_spec=scalar_grid(
            (count,),
            [
                source,
                source,
                source,
                pl.BlockSpec(
                    (level_weights.shape[0], HEAD_BLOCK, tile),
                    lambda i, p: (0, (start + i) % blocks, (start + i) // blocks),
                ),
                pl.BlockSpec((heads, dim, dim), lambda i, p: (0, 0, 0)),
            ],
            [
                pl.BlockSpec((None, HEAD_BLOCK, dim, tile), lambda i, p: (i, 0, 0, 0)),
                pl.BlockSpec((None, HEAD_BLOCK, tile, dim), lambda i, p: (i, 0, 0, 0)),
            ],
        ),
        out_shape=[
            pltpu.HBM((count, HEAD_BLOCK, dim, tile), F32),
            pltpu.HBM((count, HEAD_BLOCK, tile, dim), BF16),
        ],
        compiler_params=pltpu.CompilerParams(vmem_limit_bytes=LOCAL_VMEM),
        cost_estimate=pl.CostEstimate(
            flops=4 * count * tile * tile * HEAD_BLOCK * dim,
            bytes_accessed=12 * count * tile * HEAD_BLOCK * dim,
            transcendentals=0,
        ),
    )(place, queries, key_vectors, value_vectors, level_weights, first)


def gain_row(place, level, bit):
    scale = 2.0 ** (-0.5 * level)
    return [(level, scale if bit is None else scale * (place >> bit & 1).astype(F32))]


def bucket_sum(place, block, w_ref, q_ref, h, refs, rows):
    quarter = refs[0].shape[0] // 4
    spot = block * q_ref.shape[0] + h
    stack = [ref[(spot // quarter ^ (place & 3)) * quarter + spot % quarter] for ref in refs]
    wide = dot_nt(jnp.concatenate(stack, axis=0), q_ref[h])
    dim = stack[0].shape[0]
    total = None
    for n, row in enumerate(rows):
        gain = sum(w_ref[l, h : h + 1, :] * c for l, c in row)
        part = wide[n * dim : (n + 1) * dim] * gain
        total = part if total is None else total + part
    return total


def merge_kernel(levels, blocks, split, place_ref, qa_ref, qb_ref, aa_ref, ab_ref, w_ref, *rest):
    refs, (acc_ref, qh_ref) = rest[:-2], rest[-2:]
    rows = [gain_row(place_ref[0], *level) for level in levels]
    unit = pl.program_id(0)

    def take(q_ref, a_ref):
        qh_ref[...] = q_ref[...]
        for h in range(q_ref.shape[0]):
            acc_ref[h] = a_ref[h] + bucket_sum(
                place_ref[0], unit % blocks, w_ref, q_ref, h, refs, rows
            )

    pl.when(unit < split)(lambda: take(qa_ref, aa_ref))
    pl.when(unit >= split)(lambda: take(qb_ref, ab_ref))


def merge_part(place, turned, accs, level_weights, buckets, levels):
    split, block, tile, dim = turned[0].shape
    units = split + turned[1].shape[0]
    blocks = units // 2
    heads = block * blocks
    ahead = lambda i, p: (jnp.minimum(i, split - 1), 0, 0, 0)
    after = lambda i, p: (jnp.maximum(i - split, 0), 0, 0, 0)
    each = lambda i, p: (i, 0, 0, 0)
    return pl.pallas_call(
        functools.partial(merge_kernel, levels, blocks, split),
        grid_spec=scalar_grid(
            (units,),
            [
                pl.BlockSpec((None, block, tile, dim), ahead),
                pl.BlockSpec((None, block, tile, dim), after),
                pl.BlockSpec((None, block, dim, tile), ahead),
                pl.BlockSpec((None, block, dim, tile), after),
                pl.BlockSpec(
                    (level_weights.shape[0], block, tile), lambda i, p: (0, i % blocks, i // blocks)
                ),
            ]
            + [pl.BlockSpec((heads, dim, dim), lambda i, p: (0, 0, 0))] * len(buckets),
            [
                pl.BlockSpec((None, block, dim, tile), each),
                pl.BlockSpec((None, block, tile, dim), each),
            ],
        ),
        out_shape=[
            MERGE_SPACE((units, block, dim, tile), F32),
            MERGE_SPACE((units, block, tile, dim), BF16),
        ],
        name="merge",
        compiler_params=pltpu.CompilerParams(vmem_limit_bytes=MERGE_VMEM),
        cost_estimate=pl.CostEstimate(
            flops=2 * len(buckets) * units * block * tile * dim * dim,
            bytes_accessed=12 * units * block * tile * dim,
            transcendentals=0,
        ),
    )(place, *turned, *accs, level_weights, *buckets)


def final_kernel(meta, place_ref, q_ref, a_ref, w_ref, *rest):
    refs, out_ref = rest[:-1], rest[-1]
    above, low, top, blocks = meta
    place = place_ref[0]
    bit = lambda g: (place >> g & 1).astype(F32)
    level = lambda g, c: (above + g, c * 2.0 ** (-0.5 * (above + g)))
    rows = [gain_row(place, above + g, g) for g in range(2, top) if g != low]
    rows.append([level(low, bit(low)), level(top, bit(top) * (1.0 - bit(low)))])
    rows.append([level(top, bit(top) * bit(low))])
    done = []
    for h in range(q_ref.shape[0]):
        total = a_ref[h] + bucket_sum(
            place, pl.program_id(0) % blocks, w_ref, q_ref, h, refs, rows
        )
        done.append(total.T.astype(BF16))
    out_ref[...] = jnp.swapaxes(jnp.stack(done), 0, 1)


def final_part(place, turned, acc, level_weights, buckets, low, top):
    units, block, tile, dim = turned.shape
    blocks = units // 2
    heads = block * blocks
    each = lambda i, p: (i, 0, 0, 0)
    return pl.pallas_call(
        functools.partial(final_kernel, ((2 * tile).bit_length(), low, top, blocks)),
        grid_spec=scalar_grid(
            (units,),
            [
                pl.BlockSpec((None, block, tile, dim), each),
                pl.BlockSpec((None, block, dim, tile), each),
                pl.BlockSpec(
                    (level_weights.shape[0], block, tile), lambda i, p: (0, i % blocks, i // blocks)
                ),
            ]
            + [pl.BlockSpec((heads, dim, dim), lambda i, p: (0, 0, 0))] * len(buckets),
            pl.BlockSpec((tile, block, dim), lambda i, p: (i // blocks, i % blocks, 0)),
        ),
        out_shape=jax.ShapeDtypeStruct((2 * tile, heads, dim), BF16),
        name="final",
        compiler_params=pltpu.CompilerParams(vmem_limit_bytes=FINAL_VMEM),
        cost_estimate=pl.CostEstimate(
            flops=2 * len(buckets) * units * block * tile * dim * dim,
            bytes_accessed=12 * units * block * tile * dim,
            transcendentals=0,
        ),
    )(place, turned, acc, level_weights, *buckets)


def exchange(value, mask):
    total = lax.axis_size("outer") * lax.axis_size("inner")
    pairs = [(i, i ^ mask) for i in range(total)]
    return lax.ppermute(value, AXES, pairs)


def exchange_states(state, place, inner_depth, depth):
    quarter = state.shape[0] // 4
    high = (place >> 1 & 1) == 1
    part = lambda m: state[m * quarter : (m + 1) * quarter]
    got = {m: exchange(part(m), m) for m in (3, 2, 1)}
    rest = exchange(jnp.concatenate([part(0), part(2), part(3)]), 1)
    zero = jnp.concatenate([got[1], rest[:quarter], rest[2 * quarter :], rest[quarter : -quarter]])
    mine = part(0).astype(F32) + got[1].astype(F32)
    other = got[2].astype(F32) + got[3].astype(F32)
    total = mine + other
    sent = total.astype(BF16)
    pieces = {1: jnp.where(high, other, mine).astype(BF16)}
    pieces[1], sent, total = lax.optimization_barrier((pieces[1], sent, total))
    for g in range(2, depth):
        pieces[g] = exchange(sent, 1 << g)
        total = total + pieces[g].astype(F32)
        sent = total.astype(BF16)

    def gather_late(g):
        a = pieces[g]
        if g % 2:
            pair = jnp.concatenate([a, exchange(a, 1)])
            return jnp.concatenate([pair, exchange(pair, 2)])
        b = exchange(a, 2)
        twin = exchange(jnp.concatenate([a, b]), 1)
        return jnp.concatenate([a, twin[:quarter], b, twin[quarter:]])

    low, top = inner_depth, depth - 1
    buckets = [zero] + [gather_late(g) for g in range(1, top) if g != low]
    chosen = jnp.where((place >> low & 1) == 1, pieces[low], pieces[top])
    got = {m: exchange(chosen, m) for m in (3, 2, 1)}
    full = jnp.concatenate([chosen, got[1], got[2], got[3]])
    buckets.append(full)
    buckets.append(exchange(full, 1 << low))
    return buckets


def per_device(queries, key_vectors, value_vectors, level_weights):
    inner_count = lax.axis_size("inner")
    inner_depth = inner_count.bit_length() - 1
    depth = inner_depth + lax.axis_size("outer").bit_length() - 1
    local_depth = queries.shape[0].bit_length() - 1
    place = lax.axis_index("outer") * inner_count + lax.axis_index("inner")
    where = place.astype(jnp.int32).reshape(1)
    far = lambda x: pltpu.with_memory_space_constraint(x, pltpu.HBM)
    queries, key_vectors, value_vectors = map(far, (queries, key_vectors, value_vectors))
    state, first = block_states(where, key_vectors, value_vectors)
    buckets = exchange_states(state, place, inner_depth, depth)
    above = local_depth + 1
    units = 2 * queries.shape[1] // HEAD_BLOCK
    given = (where, queries, key_vectors, value_vectors, level_weights, first)
    split = SPLIT * units // 4
    acc0, flat0 = local_part(0, split, *given)
    acc1, flat1 = local_part(split, units - split, *given)
    acc, flat = merge_part(
        where,
        (far(flat0), far(flat1)),
        (far(acc0), far(acc1)),
        level_weights,
        buckets[:2],
        ((above, 0), (above + 1, 1)),
    )
    return final_part(
        where, flat, acc, level_weights, buckets[2:], inner_depth, depth - 1
    )


def solution(mesh):
    placed = P(AXES, None, None)
    return jax.shard_map(
        per_device,
        mesh=mesh,
        in_specs=(placed, placed, placed, P(None, None, AXES)),
        out_specs=placed,
        check_vma=False,
    )
```

```python
import functools
import jax
import jax.numpy as jnp
from jax import lax
from jax.experimental import pallas as pl
from jax.experimental.pallas import tpu as pltpu
from jax.sharding import PartitionSpec as P

AXES = ("outer", "inner")
HEAD_BLOCK = 8
STATE_VMEM = 14 << 20
LOCAL_VMEM = 14 << 20
MERGE_VMEM = 16 << 20
FINAL_VMEM = 14 << 20
MERGE_SPACE = pltpu.VMEM
SPLIT = 3
F32, BF16 = jnp.float32, jnp.bfloat16


def dot_nt(a, b):
    return lax.dot_general(a, b, (((1,), (1,)), ((), ())), preferred_element_type=F32)


def scalar_grid(grid, in_specs, out_specs):
    return pltpu.PrefetchScalarGridSpec(
        num_scalar_prefetch=1, grid=grid, in_specs=in_specs, out_specs=out_specs
    )


def state_kernel(place_ref, k_ref, v_ref, state_ref, first_ref):
    half = k_ref.shape[0] // 2
    quarter = k_ref.shape[1] // 2
    flip = place_ref[0] & 1
    keys = jnp.swapaxes(k_ref[...], 0, 1)
    values = jnp.swapaxes(v_ref[...], 0, 1)
    for h in range(2 * quarter):
        turned = values[h].T
        first = jnp.dot(turned[:, :half], keys[h, :half], preferred_element_type=F32)
        rest = jnp.dot(turned[:, half:], keys[h, half:], preferred_element_type=F32)
        spot = (h // quarter ^ flip) * quarter + h % quarter
        first_ref[spot] = first.astype(BF16)
        state_ref[spot] = (first + rest).astype(BF16)


def block_states(place, key_vectors, value_vectors):
    tokens, heads, dim = key_vectors.shape
    block = heads // 2
    source = pl.BlockSpec((tokens, block, dim), lambda i, p: (0, i ^ (p[0] >> 1 & 1), 0))
    shape = jax.ShapeDtypeStruct((heads, dim, dim), BF16)
    return pl.pallas_call(
        state_kernel,
        grid_spec=scalar_grid(
            (2,),
            [source, source],
            [pl.BlockSpec((block, dim, dim), lambda i, p: (i, 0, 0))] * 2,
        ),
        out_shape=[shape, shape],
        name="states",
        compiler_params=pltpu.CompilerParams(vmem_limit_bytes=STATE_VMEM),
        cost_estimate=pl.CostEstimate(
            flops=2 * tokens * heads * dim * dim,
            bytes_accessed=4 * tokens * heads * dim,
            transcendentals=0,
        ),
    )(place, key_vectors, value_vectors)


def local_kernel(start, blocks, place_ref, q_ref, k_ref, v_ref, w_ref, first_ref, acc_ref, qh_ref):
    unit = start + pl.program_id(0)
    second = (unit >= blocks).astype(F32)
    tile = q_ref.shape[0]
    depth = tile.bit_length() - 1
    groups = tile // 8
    queries = jnp.swapaxes(q_ref[...], 0, 1)
    keys = jnp.swapaxes(k_ref[...], 0, 1)
    values = jnp.swapaxes(v_ref[...], 0, 1)
    heads = queries.shape[0]
    lane = lax.broadcasted_iota(jnp.int32, (8, tile), 1)
    row = lax.broadcasted_iota(jnp.int32, (8, tile), 0)
    fine = (lane & 7) ^ row
    fine_ok = row <= (lane & 7)
    group_lane = lax.broadcasted_iota(jnp.int32, (groups, tile), 1) >> 3
    group_row = lax.broadcasted_iota(jnp.int32, (groups, tile), 0)
    coarse = jnp.where(group_row < group_lane, group_lane ^ group_row, 0)

    def gain(l, h):
        return w_ref[l, h : h + 1, :] * (2.0 ** (-0.5 * l))

    def weigh(h, scores):
        near = jnp.where(fine == 0, gain(0, h), 0.0)
        for l in range(1, 4):
            near = jnp.where((fine >> (l - 1)) == 1, gain(l, h), near)
        near = jnp.where(fine_ok, near, 0.0)
        far = jnp.zeros((groups, tile), F32)
        for l in range(4, depth + 1):
            far = jnp.where((coarse >> (l - 4)) == 1, gain(l, h), far)
        rows = []
        for g in range(0, groups, 2):
            pair = [
                jnp.where(
                    (lane >> 3) == g + i,
                    near,
                    jnp.broadcast_to(far[g + i : g + i + 1, :], (8, tile)),
                )
                * scores[8 * (g + i) : 8 * (g + i) + 8, :]
                for i in range(2)
            ]
            rows.append(jnp.concatenate(pair, axis=0).astype(BF16))
        return jnp.concatenate(rows, axis=0)

    scores, weights = {}, {}
    for h in range(heads + 2):
        if h < heads:
            scores[h] = dot_nt(keys[h], queries[h])
            qh_ref[h] = queries[h]
        if 0 <= h - 1 < heads:
            weights[h - 1] = weigh(h - 1, scores.pop(h - 1))
        if h - 2 >= 0:
            n = h - 2
            out = jnp.dot(values[n].T, weights.pop(n), preferred_element_type=F32)
            last = [(depth + 1, 2.0 ** (-0.5 * (depth + 1)) * second)]
            acc_ref[n] = out + bucket_sum(
                place_ref[0], unit % blocks, w_ref, queries, n, [first_ref], [last]
            )


def local_part(start, count, place, queries, key_vectors, value_vectors, level_weights, first):
    tokens, heads, dim = queries.shape
    tile = tokens // 2
    blocks = heads // HEAD_BLOCK
    source = pl.BlockSpec(
        (tile, HEAD_BLOCK, dim), lambda i, p: ((start + i) // blocks, (start + i) % blocks, 0)
    )
    return pl.pallas_call(
        functools.partial(local_kernel, start, blocks),
        grid_spec=scalar_grid(
            (count,),
            [
                source,
                source,
                source,
                pl.BlockSpec(
                    (level_weights.shape[0], HEAD_BLOCK, tile),
                    lambda i, p: (0, (start + i) % blocks, (start + i) // blocks),
                ),
                pl.BlockSpec((heads, dim, dim), lambda i, p: (0, 0, 0)),
            ],
            [
                pl.BlockSpec((None, HEAD_BLOCK, dim, tile), lambda i, p: (i, 0, 0, 0)),
                pl.BlockSpec((None, HEAD_BLOCK, tile, dim), lambda i, p: (i, 0, 0, 0)),
            ],
        ),
        out_shape=[
            pltpu.HBM((count, HEAD_BLOCK, dim, tile), F32),
            pltpu.HBM((count, HEAD_BLOCK, tile, dim), BF16),
        ],
        compiler_params=pltpu.CompilerParams(vmem_limit_bytes=LOCAL_VMEM),
        cost_estimate=pl.CostEstimate(
            flops=4 * count * tile * tile * HEAD_BLOCK * dim,
            bytes_accessed=12 * count * tile * HEAD_BLOCK * dim,
            transcendentals=0,
        ),
    )(place, queries, key_vectors, value_vectors, level_weights, first)


def gain_row(place, level, bit):
    scale = 2.0 ** (-0.5 * level)
    return [(level, scale if bit is None else scale * (place >> bit & 1).astype(F32))]


def bucket_sum(place, block, w_ref, q_ref, h, refs, rows):
    quarter = refs[0].shape[0] // 4
    spot = block * q_ref.shape[0] + h
    stack = [ref[(spot // quarter ^ (place & 3)) * quarter + spot % quarter] for ref in refs]
    wide = dot_nt(jnp.concatenate(stack, axis=0), q_ref[h])
    dim = stack[0].shape[0]
    total = None
    for n, row in enumerate(rows):
        gain = sum(w_ref[l, h : h + 1, :] * c for l, c in row)
        part = wide[n * dim : (n + 1) * dim] * gain
        total = part if total is None else total + part
    return total


def merge_kernel(levels, late, blocks, split, place_ref, qa_ref, qb_ref, aa_ref, ab_ref, w_ref, *rest):
    refs, (acc_ref, scaled_ref) = rest[:-2], rest[-2:]
    place = place_ref[0]
    rows = [gain_row(place, *level) for level in levels]
    above, low, top = late
    bit = lambda g: (place >> g & 1).astype(F32)
    level = lambda g, c: (above + g, c * 2.0 ** (-0.5 * (above + g)))
    tail = [gain_row(place, above + g, g) for g in range(2, top) if g != low]
    tail.append([level(low, bit(low)), level(top, bit(top) * (1.0 - bit(low)))])
    tail.append([level(top, bit(top) * bit(low))])
    unit = pl.program_id(0)

    def take(q_ref, a_ref):
        dim = q_ref.shape[2]
        for h in range(q_ref.shape[0]):
            acc_ref[unit, h] = a_ref[h] + bucket_sum(
                place, unit % blocks, w_ref, q_ref, h, refs, rows
            )
            turned = q_ref[h].T.astype(F32)
            for n, row in enumerate(tail):
                gain = sum(w_ref[l, h : h + 1, :] * c for l, c in row)
                scaled_ref[unit, h, n * dim : (n + 1) * dim, :] = (turned * gain).astype(BF16)

    pl.when(unit < split)(lambda: take(qa_ref, aa_ref))
    pl.when(unit >= split)(lambda: take(qb_ref, ab_ref))


def merge_part(place, turned, accs, level_weights, buckets, levels, late, count):
    split, block, tile, dim = turned[0].shape
    units = split + turned[1].shape[0]
    blocks = units // 2
    ahead = lambda i, p: (jnp.minimum(i, split - 1), 0, 0, 0)
    after = lambda i, p: (jnp.maximum(i - split, 0), 0, 0, 0)
    whole = pl.BlockSpec(memory_space=pltpu.VMEM)
    return pl.pallas_call(
        functools.partial(merge_kernel, levels, late, blocks, split),
        grid_spec=scalar_grid(
            (units,),
            [
                pl.BlockSpec((None, block, tile, dim), ahead),
                pl.BlockSpec((None, block, tile, dim), after),
                pl.BlockSpec((None, block, dim, tile), ahead),
                pl.BlockSpec((None, block, dim, tile), after),
                pl.BlockSpec(
                    (level_weights.shape[0], block, tile), lambda i, p: (0, i % blocks, i // blocks)
                ),
            ]
            + [whole] * len(buckets),
            [whole, whole],
        ),
        out_shape=[
            MERGE_SPACE((units, block, dim, tile), F32),
            MERGE_SPACE((units, block, count * dim, tile), BF16),
        ],
        name="merge",
        compiler_params=pltpu.CompilerParams(vmem_limit_bytes=MERGE_VMEM),
        cost_estimate=pl.CostEstimate(
            flops=2 * len(buckets) * units * block * tile * dim * dim,
            bytes_accessed=12 * units * block * tile * dim,
            transcendentals=0,
        ),
    )(place, *turned, *accs, level_weights, *buckets)


def final_kernel(blocks, place_ref, scaled_ref, a_ref, *rest):
    refs, out_ref = rest[:-1], rest[-1]
    unit = pl.program_id(0)
    block = scaled_ref.shape[1]
    quarter = refs[0].shape[0] // 4
    done = []
    for h in range(block):
        spot = unit % blocks * block + h
        spot = (spot // quarter ^ (place_ref[0] & 3)) * quarter + spot % quarter
        wide = jnp.concatenate([ref[spot] for ref in refs], axis=1)
        total = a_ref[unit, h] + jnp.dot(wide, scaled_ref[unit, h], preferred_element_type=F32)
        done.append(total.T.astype(BF16))
    out_ref[...] = jnp.swapaxes(jnp.stack(done), 0, 1)


def final_part(place, scaled, acc, buckets):
    units, block, dim, tile = acc.shape
    blocks = units // 2
    heads = block * blocks
    whole = pl.BlockSpec(memory_space=pltpu.VMEM)
    return pl.pallas_call(
        functools.partial(final_kernel, blocks),
        grid_spec=scalar_grid(
            (units,),
            [whole, whole] + [whole] * len(buckets),
            pl.BlockSpec((tile, block, dim), lambda i, p: (i // blocks, i % blocks, 0)),
        ),
        out_shape=jax.ShapeDtypeStruct((2 * tile, heads, dim), BF16),
        name="final",
        compiler_params=pltpu.CompilerParams(vmem_limit_bytes=FINAL_VMEM),
        cost_estimate=pl.CostEstimate(
            flops=2 * len(buckets) * units * block * tile * dim * dim,
            bytes_accessed=12 * units * block * tile * dim,
            transcendentals=0,
        ),
    )(place, scaled, acc, *buckets)


def exchange(value, mask):
    total = lax.axis_size("outer") * lax.axis_size("inner")
    pairs = [(i, i ^ mask) for i in range(total)]
    return lax.ppermute(value, AXES, pairs)


def exchange_states(state, place, inner_depth, depth):
    quarter = state.shape[0] // 4
    high = (place >> 1 & 1) == 1
    part = lambda m: state[m * quarter : (m + 1) * quarter]
    got = {m: exchange(part(m), m) for m in (3, 2, 1)}
    rest = exchange(jnp.concatenate([part(0), part(2), part(3)]), 1)
    zero = jnp.concatenate([got[1], rest[:quarter], rest[2 * quarter :], rest[quarter : -quarter]])
    mine = part(0).astype(F32) + got[1].astype(F32)
    other = got[2].astype(F32) + got[3].astype(F32)
    total = mine + other
    sent = total.astype(BF16)
    pieces = {1: jnp.where(high, other, mine).astype(BF16)}
    pieces[1], sent, total = lax.optimization_barrier((pieces[1], sent, total))
    for g in range(2, depth):
        pieces[g] = exchange(sent, 1 << g)
        total = total + pieces[g].astype(F32)
        sent = total.astype(BF16)

    def gather_late(g):
        a = pieces[g]
        if g % 2:
            pair = jnp.concatenate([a, exchange(a, 1)])
            return jnp.concatenate([pair, exchange(pair, 2)])
        b = exchange(a, 2)
        twin = exchange(jnp.concatenate([a, b]), 1)
        return jnp.concatenate([a, twin[:quarter], b, twin[quarter:]])

    low, top = inner_depth, depth - 1
    buckets = [zero] + [gather_late(g) for g in range(1, top) if g != low]
    chosen = jnp.where((place >> low & 1) == 1, pieces[low], pieces[top])
    got = {m: exchange(chosen, m) for m in (3, 2, 1)}
    full = jnp.concatenate([chosen, got[1], got[2], got[3]])
    buckets.append(full)
    buckets.append(exchange(full, 1 << low))
    return buckets


def per_device(queries, key_vectors, value_vectors, level_weights):
    inner_count = lax.axis_size("inner")
    inner_depth = inner_count.bit_length() - 1
    depth = inner_depth + lax.axis_size("outer").bit_length() - 1
    local_depth = queries.shape[0].bit_length() - 1
    place = lax.axis_index("outer") * inner_count + lax.axis_index("inner")
    where = place.astype(jnp.int32).reshape(1)
    far = lambda x: pltpu.with_memory_space_constraint(x, pltpu.HBM)
    queries, key_vectors, value_vectors = map(far, (queries, key_vectors, value_vectors))
    state, first = block_states(where, key_vectors, value_vectors)
    buckets = exchange_states(state, place, inner_depth, depth)
    above = local_depth + 1
    units = 2 * queries.shape[1] // HEAD_BLOCK
    given = (where, queries, key_vectors, value_vectors, level_weights, first)
    split = SPLIT * units // 4
    acc0, flat0 = local_part(0, split, *given)
    acc1, flat1 = local_part(split, units - split, *given)
    acc, scaled = merge_part(
        where,
        (far(flat0), far(flat1)),
        (far(acc0), far(acc1)),
        level_weights,
        buckets[:2],
        ((above, 0), (above + 1, 1)),
        (above, inner_depth, depth - 1),
        len(buckets) - 2,
    )
    return final_part(where, scaled, acc, buckets[2:])


def solution(mesh):
    placed = P(AXES, None, None)
    return jax.shard_map(
        per_device,
        mesh=mesh,
        in_specs=(placed, placed, placed, P(None, None, AXES)),
        out_specs=placed,
        check_vma=False,
    )
```

```python
import functools
import jax
import jax.numpy as jnp
from jax import lax
from jax.experimental import pallas as pl
from jax.experimental.pallas import tpu as pltpu
from jax.sharding import PartitionSpec as P

AXES = ("outer", "inner")
HEAD_BLOCK = 8
STATE_VMEM = 14 << 20
LOCAL_VMEM = 14 << 20
MERGE_VMEM = 16 << 20
FINAL_VMEM = 14 << 20
MERGE_SPACE = pltpu.VMEM
SPLIT = 3
F32, BF16 = jnp.float32, jnp.bfloat16


def dot_nt(a, b):
    return lax.dot_general(a, b, (((1,), (1,)), ((), ())), preferred_element_type=F32)


def scalar_grid(grid, in_specs, out_specs):
    return pltpu.PrefetchScalarGridSpec(
        num_scalar_prefetch=1, grid=grid, in_specs=in_specs, out_specs=out_specs
    )


def state_kernel(place_ref, k_ref, v_ref, state_ref, first_ref):
    half = k_ref.shape[0] // 2
    quarter = k_ref.shape[1] // 2
    flip = place_ref[0] & 1
    keys = jnp.swapaxes(k_ref[...], 0, 1)
    values = jnp.swapaxes(v_ref[...], 0, 1)
    for h in range(2 * quarter):
        turned = values[h].T
        first = jnp.dot(turned[:, :half], keys[h, :half], preferred_element_type=F32)
        rest = jnp.dot(turned[:, half:], keys[h, half:], preferred_element_type=F32)
        spot = (h // quarter ^ flip) * quarter + h % quarter
        first_ref[spot] = first.astype(BF16)
        state_ref[spot] = (first + rest).astype(BF16)


def block_states(place, key_vectors, value_vectors):
    tokens, heads, dim = key_vectors.shape
    block = heads // 2
    source = pl.BlockSpec((tokens, block, dim), lambda i, p: (0, i ^ (p[0] >> 1 & 1), 0))
    shape = jax.ShapeDtypeStruct((heads, dim, dim), BF16)
    return pl.pallas_call(
        state_kernel,
        grid_spec=scalar_grid(
            (2,),
            [source, source],
            [pl.BlockSpec((block, dim, dim), lambda i, p: (i, 0, 0))] * 2,
        ),
        out_shape=[shape, shape],
        name="states",
        compiler_params=pltpu.CompilerParams(vmem_limit_bytes=STATE_VMEM),
        cost_estimate=pl.CostEstimate(
            flops=2 * tokens * heads * dim * dim,
            bytes_accessed=4 * tokens * heads * dim,
            transcendentals=0,
        ),
    )(place, key_vectors, value_vectors)


def local_kernel(start, blocks, place_ref, q_ref, k_ref, v_ref, w_ref, first_ref, acc_ref, qh_ref):
    unit = start + pl.program_id(0)
    second = (unit >= blocks).astype(F32)
    tile = q_ref.shape[0]
    depth = tile.bit_length() - 1
    groups = tile // 8
    queries = jnp.swapaxes(q_ref[...], 0, 1)
    keys = jnp.swapaxes(k_ref[...], 0, 1)
    values = jnp.swapaxes(v_ref[...], 0, 1)
    heads = queries.shape[0]
    lane = lax.broadcasted_iota(jnp.int32, (8, tile), 1)
    row = lax.broadcasted_iota(jnp.int32, (8, tile), 0)
    fine = (lane & 7) ^ row
    fine_ok = row <= (lane & 7)
    group_lane = lax.broadcasted_iota(jnp.int32, (groups, tile), 1) >> 3
    group_row = lax.broadcasted_iota(jnp.int32, (groups, tile), 0)
    coarse = jnp.where(group_row < group_lane, group_lane ^ group_row, 0)

    def gain(l, h):
        return w_ref[l, h : h + 1, :] * (2.0 ** (-0.5 * l))

    def weigh(h, scores):
        near = jnp.where(fine == 0, gain(0, h), 0.0)
        for l in range(1, 4):
            near = jnp.where((fine >> (l - 1)) == 1, gain(l, h), near)
        near = jnp.where(fine_ok, near, 0.0)
        far = jnp.zeros((groups, tile), F32)
        for l in range(4, depth + 1):
            far = jnp.where((coarse >> (l - 4)) == 1, gain(l, h), far)
        rows = []
        for g in range(0, groups, 2):
            pair = [
                jnp.where(
                    (lane >> 3) == g + i,
                    near,
                    jnp.broadcast_to(far[g + i : g + i + 1, :], (8, tile)),
                )
                * scores[8 * (g + i) : 8 * (g + i) + 8, :]
                for i in range(2)
            ]
            rows.append(jnp.concatenate(pair, axis=0).astype(BF16))
        return jnp.concatenate(rows, axis=0)

    scores, weights = {}, {}
    for h in range(heads + 2):
        if h < heads:
            scores[h] = dot_nt(keys[h], queries[h])
            qh_ref[h] = queries[h]
        if 0 <= h - 1 < heads:
            weights[h - 1] = weigh(h - 1, scores.pop(h - 1))
        if h - 2 >= 0:
            n = h - 2
            out = jnp.dot(values[n].T, weights.pop(n), preferred_element_type=F32)
            last = [(depth + 1, 2.0 ** (-0.5 * (depth + 1)) * second)]
            acc_ref[n] = out + bucket_sum(
                place_ref[0], unit % blocks, w_ref, queries, n, [first_ref], [last]
            )


def local_part(start, count, place, queries, key_vectors, value_vectors, level_weights, first):
    tokens, heads, dim = queries.shape
    tile = tokens // 2
    blocks = heads // HEAD_BLOCK
    source = pl.BlockSpec(
        (tile, HEAD_BLOCK, dim), lambda i, p: ((start + i) // blocks, (start + i) % blocks, 0)
    )
    return pl.pallas_call(
        functools.partial(local_kernel, start, blocks),
        grid_spec=scalar_grid(
            (count,),
            [
                source,
                source,
                source,
                pl.BlockSpec(
                    (level_weights.shape[0], HEAD_BLOCK, tile),
                    lambda i, p: (0, (start + i) % blocks, (start + i) // blocks),
                ),
                pl.BlockSpec((heads, dim, dim), lambda i, p: (0, 0, 0)),
            ],
            [
                pl.BlockSpec((None, HEAD_BLOCK, dim, tile), lambda i, p: (i, 0, 0, 0)),
                pl.BlockSpec((None, HEAD_BLOCK, tile, dim), lambda i, p: (i, 0, 0, 0)),
            ],
        ),
        out_shape=[
            pltpu.HBM((count, HEAD_BLOCK, dim, tile), F32),
            pltpu.HBM((count, HEAD_BLOCK, tile, dim), BF16),
        ],
        compiler_params=pltpu.CompilerParams(vmem_limit_bytes=LOCAL_VMEM),
        cost_estimate=pl.CostEstimate(
            flops=4 * count * tile * tile * HEAD_BLOCK * dim,
            bytes_accessed=12 * count * tile * HEAD_BLOCK * dim,
            transcendentals=0,
        ),
    )(place, queries, key_vectors, value_vectors, level_weights, first)


def gain_row(place, level, bit):
    scale = 2.0 ** (-0.5 * level)
    return [(level, scale if bit is None else scale * (place >> bit & 1).astype(F32))]


def bucket_sum(place, block, w_ref, q_ref, h, refs, rows):
    quarter = refs[0].shape[0] // 4
    spot = block * q_ref.shape[0] + h
    stack = [ref[(spot // quarter ^ (place & 3)) * quarter + spot % quarter] for ref in refs]
    wide = dot_nt(jnp.concatenate(stack, axis=0), q_ref[h])
    dim = stack[0].shape[0]
    total = None
    for n, row in enumerate(rows):
        gain = sum(w_ref[l, h : h + 1, :] * c for l, c in row)
        part = wide[n * dim : (n + 1) * dim] * gain
        total = part if total is None else total + part
    return total


def merge_kernel(levels, late, blocks, split, place_ref, qa_ref, qb_ref, aa_ref, ab_ref, w_ref, *rest):
    refs, (acc_ref, scaled_ref) = rest[:-2], rest[-2:]
    place = place_ref[0]
    rows = [gain_row(place, *level) for level in levels]
    above, low, top = late
    bit = lambda g: (place >> g & 1).astype(F32)
    level = lambda g, c: (above + g, c * 2.0 ** (-0.5 * (above + g)))
    tail = [gain_row(place, above + g, g) for g in range(1, top) if g != low]
    tail.append([level(low, bit(low)), level(top, bit(top) * (1.0 - bit(low)))])
    tail.append([level(top, bit(top) * bit(low))])
    unit = pl.program_id(0)

    def take(q_ref, a_ref):
        dim = q_ref.shape[2]
        for h in range(q_ref.shape[0]):
            acc_ref[unit, h] = a_ref[h] + bucket_sum(
                place, unit % blocks, w_ref, q_ref, h, refs, rows
            )
            turned = q_ref[h].T.astype(F32)
            for n, row in enumerate(tail):
                gain = sum(w_ref[l, h : h + 1, :] * c for l, c in row)
                scaled_ref[unit, h, n * dim : (n + 1) * dim, :] = (turned * gain).astype(BF16)

    pl.when(unit < split)(lambda: take(qa_ref, aa_ref))
    pl.when(unit >= split)(lambda: take(qb_ref, ab_ref))


def merge_part(place, turned, accs, level_weights, buckets, levels, late, count):
    split, block, tile, dim = turned[0].shape
    units = split + turned[1].shape[0]
    blocks = units // 2
    ahead = lambda i, p: (jnp.minimum(i, split - 1), 0, 0, 0)
    after = lambda i, p: (jnp.maximum(i - split, 0), 0, 0, 0)
    whole = pl.BlockSpec(memory_space=pltpu.VMEM)
    return pl.pallas_call(
        functools.partial(merge_kernel, levels, late, blocks, split),
        grid_spec=scalar_grid(
            (units,),
            [
                pl.BlockSpec((None, block, tile, dim), ahead),
                pl.BlockSpec((None, block, tile, dim), after),
                pl.BlockSpec((None, block, dim, tile), ahead),
                pl.BlockSpec((None, block, dim, tile), after),
                pl.BlockSpec(
                    (level_weights.shape[0], block, tile), lambda i, p: (0, i % blocks, i // blocks)
                ),
            ]
            + [whole] * len(buckets),
            [whole, whole],
        ),
        out_shape=[
            MERGE_SPACE((units, block, dim, tile), F32),
            MERGE_SPACE((units, block, count * dim, tile), BF16),
        ],
        name="merge",
        compiler_params=pltpu.CompilerParams(vmem_limit_bytes=MERGE_VMEM),
        cost_estimate=pl.CostEstimate(
            flops=2 * len(buckets) * units * block * tile * dim * dim,
            bytes_accessed=12 * units * block * tile * dim,
            transcendentals=0,
        ),
    )(place, *turned, *accs, level_weights, *buckets)


def final_kernel(blocks, part, place_ref, scaled_ref, a_ref, *rest):
    refs, out_ref = rest[:-1], rest[-1]
    place = place_ref[0]
    unit = pl.program_id(0) * blocks + ((place >> 1 & 1) ^ part)
    block = scaled_ref.shape[1]
    quarter = block // 2
    if part:
        refs = refs[:-1]
    done = []
    for h in range(block):
        spot = (h // quarter ^ (place & 1)) * quarter + h % quarter
        wide = jnp.concatenate([ref[spot] for ref in refs], axis=1)
        total = a_ref[unit, h] + jnp.dot(wide, scaled_ref[unit, h], preferred_element_type=F32)
        done.append(total.T.astype(BF16))
    out_ref[...] = jnp.swapaxes(jnp.stack(done), 0, 1)


def final_part(part, place, scaled, acc, buckets, before):
    units, block, dim, tile = acc.shape
    blocks = units // 2
    whole = pl.BlockSpec(memory_space=pltpu.VMEM)
    kept = [] if before is None else [before]
    return pl.pallas_call(
        functools.partial(final_kernel, blocks, part),
        grid_spec=scalar_grid(
            (2,),
            [whole, whole]
            + [whole] * len(buckets)
            + [pl.BlockSpec(memory_space=pl.ANY)] * len(kept),
            pl.BlockSpec((tile, block, dim), lambda i, p: (i, (p[0] >> 1 & 1) ^ part, 0)),
        ),
        out_shape=jax.ShapeDtypeStruct((2 * tile, blocks * block, dim), BF16),
        input_output_aliases={3 + len(buckets): 0} if kept else {},
        compiler_params=pltpu.CompilerParams(vmem_limit_bytes=FINAL_VMEM),
        cost_estimate=pl.CostEstimate(
            flops=len(buckets) * units * block * tile * dim * dim,
            bytes_accessed=6 * units * block * tile * dim,
            transcendentals=0,
        ),
    )(place, scaled, acc, *buckets, *kept)


def exchange(value, mask):
    total = lax.axis_size("outer") * lax.axis_size("inner")
    pairs = [(i, i ^ mask) for i in range(total)]
    return lax.ppermute(value, AXES, pairs)


def exchange_states(state, place, inner_depth, depth):
    quarter = state.shape[0] // 4
    high = (place >> 1 & 1) == 1
    part = lambda m: state[m * quarter : (m + 1) * quarter]
    got = {m: exchange(part(m), m) for m in (3, 2, 1)}
    rest = exchange(jnp.concatenate([part(0), part(2), part(3)]), 1)
    zero = jnp.concatenate([got[1], rest[:quarter], rest[2 * quarter :], rest[quarter : -quarter]])
    mine = part(0).astype(F32) + got[1].astype(F32)
    other = got[2].astype(F32) + got[3].astype(F32)
    total = mine + other
    sent = total.astype(BF16)
    pieces = {1: jnp.where(high, other, mine).astype(BF16)}
    pieces[1], sent, total = lax.optimization_barrier((pieces[1], sent, total))
    for g in range(2, depth):
        pieces[g] = exchange(sent, 1 << g)
        total = total + pieces[g].astype(F32)
        sent = total.astype(BF16)

    def gather_late(g):
        a = pieces[g]
        twin = exchange(a, 1)
        pair = jnp.concatenate([a, twin])
        return pair, exchange(pair, 2)

    low, top = inner_depth, depth - 1
    buckets = [gather_late(g) for g in range(1, top) if g != low]
    chosen = jnp.where((place >> low & 1) == 1, pieces[low], pieces[top])
    got = {m: exchange(chosen, m) for m in (1, 3, 2)}
    full = jnp.concatenate([chosen, got[1]]), jnp.concatenate([got[2], got[3]])
    buckets.append(full)
    buckets.append([exchange(side, 1 << low) for side in full])
    return zero, buckets


def per_device(queries, key_vectors, value_vectors, level_weights):
    inner_count = lax.axis_size("inner")
    inner_depth = inner_count.bit_length() - 1
    depth = inner_depth + lax.axis_size("outer").bit_length() - 1
    local_depth = queries.shape[0].bit_length() - 1
    place = lax.axis_index("outer") * inner_count + lax.axis_index("inner")
    where = place.astype(jnp.int32).reshape(1)
    far = lambda x: pltpu.with_memory_space_constraint(x, pltpu.HBM)
    queries, key_vectors, value_vectors = map(far, (queries, key_vectors, value_vectors))
    state, first = block_states(where, key_vectors, value_vectors)
    zero, buckets = exchange_states(state, place, inner_depth, depth)
    above = local_depth + 1
    units = 2 * queries.shape[1] // HEAD_BLOCK
    given = (where, queries, key_vectors, value_vectors, level_weights, first)
    split = SPLIT * units // 4
    acc0, flat0 = local_part(0, split, *given)
    acc1, flat1 = local_part(split, units - split, *given)
    acc, scaled = merge_part(
        where,
        (far(flat0), far(flat1)),
        (far(acc0), far(acc1)),
        level_weights,
        [zero],
        ((above, 0),),
        (above, inner_depth, depth - 1),
        len(buckets),
    )
    out = None
    for part in range(2):
        out = final_part(part, where, scaled, acc, [b[part] for b in buckets], out)
    return out


def solution(mesh):
    placed = P(AXES, None, None)
    return jax.shard_map(
        per_device,
        mesh=mesh,
        in_specs=(placed, placed, placed, P(None, None, AXES)),
        out_specs=placed,
        check_vma=False,
    )
```

```python
import functools
import jax
import jax.numpy as jnp
from jax import lax
from jax.experimental import pallas as pl
from jax.experimental.pallas import tpu as pltpu
from jax.sharding import PartitionSpec as P

AXES = ("outer", "inner")
HEAD_BLOCK = 8
STATE_VMEM = 14 << 20
LOCAL_VMEM = 14 << 20
MERGE_VMEM = 16 << 20
FINAL_VMEM = 14 << 20
MERGE_SPACE = pltpu.VMEM
SPLIT = 3
F32, BF16 = jnp.float32, jnp.bfloat16


def dot_nt(a, b):
    return lax.dot_general(a, b, (((1,), (1,)), ((), ())), preferred_element_type=F32)


def scalar_grid(grid, in_specs, out_specs):
    return pltpu.PrefetchScalarGridSpec(
        num_scalar_prefetch=1, grid=grid, in_specs=in_specs, out_specs=out_specs
    )


def state_kernel(place_ref, k_ref, v_ref, state_ref, first_ref):
    half = k_ref.shape[0] // 2
    quarter = k_ref.shape[1] // 2
    flip = place_ref[0] & 1
    keys = jnp.swapaxes(k_ref[...], 0, 1)
    values = jnp.swapaxes(v_ref[...], 0, 1)
    for h in range(2 * quarter):
        turned = values[h].T
        first = jnp.dot(turned[:, :half], keys[h, :half], preferred_element_type=F32)
        rest = jnp.dot(turned[:, half:], keys[h, half:], preferred_element_type=F32)
        spot = (h // quarter ^ flip) * quarter + h % quarter
        first_ref[spot] = first.astype(BF16)
        state_ref[spot] = (first + rest).astype(BF16)


def block_states(place, key_vectors, value_vectors):
    tokens, heads, dim = key_vectors.shape
    block = heads // 2
    source = pl.BlockSpec((tokens, block, dim), lambda i, p: (0, i ^ (p[0] >> 1 & 1), 0))
    shape = jax.ShapeDtypeStruct((heads, dim, dim), BF16)
    return pl.pallas_call(
        state_kernel,
        grid_spec=scalar_grid(
            (2,),
            [source, source],
            [pl.BlockSpec((block, dim, dim), lambda i, p: (i, 0, 0))] * 2,
        ),
        out_shape=[shape, shape],
        name="states",
        compiler_params=pltpu.CompilerParams(vmem_limit_bytes=STATE_VMEM),
        cost_estimate=pl.CostEstimate(
            flops=2 * tokens * heads * dim * dim,
            bytes_accessed=4 * tokens * heads * dim,
            transcendentals=0,
        ),
    )(place, key_vectors, value_vectors)


def local_kernel(start, blocks, place_ref, q_ref, k_ref, v_ref, w_ref, first_ref, *rest):
    acc_ref, qh_ref = rest[-2:]
    unit = start + pl.program_id(0)
    second = (unit >= blocks).astype(F32)
    tile = q_ref.shape[0]
    depth = tile.bit_length() - 1
    groups = tile // 8
    queries = jnp.swapaxes(q_ref[...], 0, 1)
    keys = jnp.swapaxes(k_ref[...], 0, 1)
    values = jnp.swapaxes(v_ref[...], 0, 1)
    heads = queries.shape[0]
    lane = lax.broadcasted_iota(jnp.int32, (8, tile), 1)
    row = lax.broadcasted_iota(jnp.int32, (8, tile), 0)
    fine = (lane & 7) ^ row
    fine_ok = row <= (lane & 7)
    group_lane = lax.broadcasted_iota(jnp.int32, (groups, tile), 1) >> 3
    group_row = lax.broadcasted_iota(jnp.int32, (groups, tile), 0)
    coarse = jnp.where(group_row < group_lane, group_lane ^ group_row, 0)

    def gain(l, h):
        return w_ref[l, h : h + 1, :] * (2.0 ** (-0.5 * l))

    def weigh(h, scores):
        near = jnp.where(fine == 0, gain(0, h), 0.0)
        for l in range(1, 4):
            near = jnp.where((fine >> (l - 1)) == 1, gain(l, h), near)
        near = jnp.where(fine_ok, near, 0.0)
        far = jnp.zeros((groups, tile), F32)
        for l in range(4, depth + 1):
            far = jnp.where((coarse >> (l - 4)) == 1, gain(l, h), far)
        rows = []
        for g in range(0, groups, 2):
            pair = [
                jnp.where(
                    (lane >> 3) == g + i,
                    near,
                    jnp.broadcast_to(far[g + i : g + i + 1, :], (8, tile)),
                )
                * scores[8 * (g + i) : 8 * (g + i) + 8, :]
                for i in range(2)
            ]
            rows.append(jnp.concatenate(pair, axis=0).astype(BF16))
        return jnp.concatenate(rows, axis=0)

    scores, weights = {}, {}
    for h in range(heads + 2):
        if h < heads:
            scores[h] = dot_nt(keys[h], queries[h])
            qh_ref[h] = queries[h]
        if 0 <= h - 1 < heads:
            weights[h - 1] = weigh(h - 1, scores.pop(h - 1))
        if h - 2 >= 0:
            n = h - 2
            out = jnp.dot(values[n].T, weights.pop(n), preferred_element_type=F32)
            last = [(depth + 1, 2.0 ** (-0.5 * (depth + 1)) * second)]
            acc_ref[n] = out + bucket_sum(
                place_ref[0], unit % blocks, w_ref, queries, n, [first_ref], [last]
            )


def local_part(start, count, place, queries, key_vectors, value_vectors, weights, first, kept=()):
    tokens, heads, dim = queries.shape
    tile = tokens // 2
    blocks = heads // HEAD_BLOCK
    units = 2 * blocks
    source = pl.BlockSpec(
        (tile, HEAD_BLOCK, dim), lambda i, p: ((start + i) // blocks, (start + i) % blocks, 0)
    )
    return pl.pallas_call(
        functools.partial(local_kernel, start, blocks),
        grid_spec=scalar_grid(
            (count,),
            [
                source,
                source,
                source,
                pl.BlockSpec(
                    (weights.shape[0], HEAD_BLOCK, tile),
                    lambda i, p: (0, (start + i) % blocks, (start + i) // blocks),
                ),
                pl.BlockSpec((heads, dim, dim), lambda i, p: (0, 0, 0)),
            ]
            + [pl.BlockSpec(memory_space=pl.ANY)] * len(kept),
            [
                pl.BlockSpec((None, HEAD_BLOCK, dim, tile), lambda i, p: (start + i, 0, 0, 0)),
                pl.BlockSpec((None, HEAD_BLOCK, tile, dim), lambda i, p: (start + i, 0, 0, 0)),
            ],
        ),
        out_shape=[
            pltpu.HBM((units, HEAD_BLOCK, dim, tile), F32),
            pltpu.HBM((units, HEAD_BLOCK, tile, dim), BF16),
        ],
        input_output_aliases={6: 0, 7: 1} if kept else {},
        compiler_params=pltpu.CompilerParams(vmem_limit_bytes=LOCAL_VMEM),
        cost_estimate=pl.CostEstimate(
            flops=4 * count * tile * tile * HEAD_BLOCK * dim,
            bytes_accessed=12 * count * tile * HEAD_BLOCK * dim,
            transcendentals=0,
        ),
    )(place, queries, key_vectors, value_vectors, weights, first, *kept)


def gain_row(place, level, bit):
    scale = 2.0 ** (-0.5 * level)
    return [(level, scale if bit is None else scale * (place >> bit & 1).astype(F32))]


def bucket_sum(place, block, w_ref, q_ref, h, refs, rows):
    quarter = refs[0].shape[0] // 4
    spot = block * q_ref.shape[0] + h
    stack = [ref[(spot // quarter ^ (place & 3)) * quarter + spot % quarter] for ref in refs]
    wide = dot_nt(jnp.concatenate(stack, axis=0), q_ref[h])
    dim = stack[0].shape[0]
    total = None
    for n, row in enumerate(rows):
        gain = sum(w_ref[l, h : h + 1, :] * c for l, c in row)
        part = wide[n * dim : (n + 1) * dim] * gain
        total = part if total is None else total + part
    return total


def merge_kernel(levels, late, blocks, place_ref, q_ref, a_ref, w_ref, *rest):
    refs, (acc_ref, scaled_ref) = rest[:-2], rest[-2:]
    place = place_ref[0]
    rows = [gain_row(place, *level) for level in levels]
    above, low, top = late
    bit = lambda g: (place >> g & 1).astype(F32)
    level = lambda g, c: (above + g, c * 2.0 ** (-0.5 * (above + g)))
    tail = [gain_row(place, above + g, g) for g in range(1, top) if g != low]
    tail.append([level(low, bit(low)), level(top, bit(top) * (1.0 - bit(low)))])
    tail.append([level(top, bit(top) * bit(low))])
    unit = pl.program_id(0)

    dim = q_ref.shape[2]
    for h in range(q_ref.shape[0]):
        acc_ref[unit, h] = a_ref[h] + bucket_sum(
            place, unit % blocks, w_ref, q_ref, h, refs, rows
        )
        turned = q_ref[h].T.astype(F32)
        for n, row in enumerate(tail):
            gain = sum(w_ref[l, h : h + 1, :] * c for l, c in row)
            scaled_ref[unit, h, n * dim : (n + 1) * dim, :] = (turned * gain).astype(BF16)


def merge_part(place, turned, acc, level_weights, buckets, levels, late, count):
    units, block, tile, dim = turned.shape
    blocks = units // 2
    each = lambda i, p: (i, 0, 0, 0)
    whole = pl.BlockSpec(memory_space=pltpu.VMEM)
    return pl.pallas_call(
        functools.partial(merge_kernel, levels, late, blocks),
        grid_spec=scalar_grid(
            (units,),
            [
                pl.BlockSpec((None, block, tile, dim), each),
                pl.BlockSpec((None, block, dim, tile), each),
                pl.BlockSpec(
                    (level_weights.shape[0], block, tile), lambda i, p: (0, i % blocks, i // blocks)
                ),
            ]
            + [whole] * len(buckets),
            [whole, whole],
        ),
        out_shape=[
            MERGE_SPACE((units, block, dim, tile), F32),
            MERGE_SPACE((units, block, count * dim, tile), BF16),
        ],
        name="merge",
        compiler_params=pltpu.CompilerParams(vmem_limit_bytes=MERGE_VMEM),
        cost_estimate=pl.CostEstimate(
            flops=2 * len(buckets) * units * block * tile * dim * dim,
            bytes_accessed=12 * units * block * tile * dim,
            transcendentals=0,
        ),
    )(place, turned, acc, level_weights, *buckets)


def final_kernel(blocks, part, place_ref, scaled_ref, a_ref, *rest):
    refs, out_ref = rest[:-1], rest[-1]
    place = place_ref[0]
    unit = pl.program_id(0) * blocks + ((place >> 1 & 1) ^ part)
    block = scaled_ref.shape[1]
    quarter = block // 2
    if part:
        refs = refs[:-1]
    done = []
    for h in range(block):
        spot = (h // quarter ^ (place & 1)) * quarter + h % quarter
        wide = jnp.concatenate([ref[spot] for ref in refs], axis=1)
        total = a_ref[unit, h] + jnp.dot(wide, scaled_ref[unit, h], preferred_element_type=F32)
        done.append(total.T.astype(BF16))
    out_ref[...] = jnp.swapaxes(jnp.stack(done), 0, 1)


def final_part(part, place, scaled, acc, buckets, before):
    units, block, dim, tile = acc.shape
    blocks = units // 2
    whole = pl.BlockSpec(memory_space=pltpu.VMEM)
    kept = [] if before is None else [before]
    return pl.pallas_call(
        functools.partial(final_kernel, blocks, part),
        grid_spec=scalar_grid(
            (2,),
            [whole, whole]
            + [whole] * len(buckets)
            + [pl.BlockSpec(memory_space=pl.ANY)] * len(kept),
            pl.BlockSpec((tile, block, dim), lambda i, p: (i, (p[0] >> 1 & 1) ^ part, 0)),
        ),
        out_shape=jax.ShapeDtypeStruct((2 * tile, blocks * block, dim), BF16),
        input_output_aliases={3 + len(buckets): 0} if kept else {},
        compiler_params=pltpu.CompilerParams(vmem_limit_bytes=FINAL_VMEM),
        cost_estimate=pl.CostEstimate(
            flops=len(buckets) * units * block * tile * dim * dim,
            bytes_accessed=6 * units * block * tile * dim,
            transcendentals=0,
        ),
    )(place, scaled, acc, *buckets, *kept)


def exchange(value, mask):
    total = lax.axis_size("outer") * lax.axis_size("inner")
    pairs = [(i, i ^ mask) for i in range(total)]
    return lax.ppermute(value, AXES, pairs)


def exchange_states(state, place, inner_depth, depth):
    quarter = state.shape[0] // 4
    high = (place >> 1 & 1) == 1
    part = lambda m: state[m * quarter : (m + 1) * quarter]
    got = {m: exchange(part(m), m) for m in (3, 2, 1)}
    rest = exchange(jnp.concatenate([part(0), part(2), part(3)]), 1)
    zero = jnp.concatenate([got[1], rest[:quarter], rest[2 * quarter :], rest[quarter : -quarter]])
    mine = part(0).astype(F32) + got[1].astype(F32)
    other = got[2].astype(F32) + got[3].astype(F32)
    total = mine + other
    sent = total.astype(BF16)
    pieces = {1: jnp.where(high, other, mine).astype(BF16)}
    pieces[1], sent, total = lax.optimization_barrier((pieces[1], sent, total))
    for g in range(2, depth):
        pieces[g] = exchange(sent, 1 << g)
        total = total + pieces[g].astype(F32)
        sent = total.astype(BF16)

    def gather_late(g):
        a = pieces[g]
        twin = exchange(a, 1)
        pair = jnp.concatenate([a, twin])
        return pair, exchange(pair, 2)

    low, top = inner_depth, depth - 1
    buckets = [gather_late(g) for g in range(1, top) if g != low]
    chosen = jnp.where((place >> low & 1) == 1, pieces[low], pieces[top])
    got = {m: exchange(chosen, m) for m in (1, 3, 2)}
    full = jnp.concatenate([chosen, got[1]]), jnp.concatenate([got[2], got[3]])
    buckets.append(full)
    buckets.append([exchange(side, 1 << low) for side in full])
    return zero, buckets


def per_device(queries, key_vectors, value_vectors, level_weights):
    inner_count = lax.axis_size("inner")
    inner_depth = inner_count.bit_length() - 1
    depth = inner_depth + lax.axis_size("outer").bit_length() - 1
    local_depth = queries.shape[0].bit_length() - 1
    place = lax.axis_index("outer") * inner_count + lax.axis_index("inner")
    where = place.astype(jnp.int32).reshape(1)
    far = lambda x: pltpu.with_memory_space_constraint(x, pltpu.HBM)
    queries, key_vectors, value_vectors = map(far, (queries, key_vectors, value_vectors))
    state, first = block_states(where, key_vectors, value_vectors)
    zero, buckets = exchange_states(state, place, inner_depth, depth)
    above = local_depth + 1
    units = 2 * queries.shape[1] // HEAD_BLOCK
    given = (where, queries, key_vectors, value_vectors, level_weights, first)
    split = SPLIT * units // 4
    sums = local_part(0, split, *given)
    acc, flat = local_part(split, units - split, *given, sums)
    acc, scaled = merge_part(
        where,
        far(flat),
        far(acc),
        level_weights,
        [zero],
        ((above, 0),),
        (above, inner_depth, depth - 1),
        len(buckets),
    )
    out = None
    for part in range(2):
        out = final_part(part, where, scaled, acc, [b[part] for b in buckets], out)
    return out


def solution(mesh):
    placed = P(AXES, None, None)
    return jax.shard_map(
        per_device,
        mesh=mesh,
        in_specs=(placed, placed, placed, P(None, None, AXES)),
        out_specs=placed,
        check_vma=False,
    )
```
